256 devices in a mesh: lat: 16 (over z, x_lo), lon: 16 (over x_hi, y, core).
Axes of the slice: x: 4 (x_hi: 2, x_lo: 2; x = x_hi * 2 + x_lo), y: 4, z: 8, core: 2. Of those that a mesh axis runs over, the one named last changes fastest.
Arguments:
- tokens: bfloat16 [128, 256, 2, 1024], P('lat', 'lon'), may hold values from -6 to 6
- norm_gain: bfloat16 [1024], replicated, may hold values from 0.099609375 to 1.8984375
- q_weight: bfloat16 [1024, 1024], replicated, may hold values from -3 to 3
- k_weight: bfloat16 [1024, 1024], replicated, may hold values from -3 to 3
- v_weight: bfloat16 [1024, 1024], replicated, may hold values from -0.1875 to 0.1875
- o_weight: bfloat16 [1024, 1024], replicated, may hold values from -0.75 to 0.75
- band_start: int32 [16], replicated, may hold values from -15 to 0, as said below
- band_width: int32 [16], replicated, may hold values from 2 to 16, as said below
Outputs:
- mixed: bfloat16 [128, 256, 2, 1024], P('lat', 'lon')
The draws below stay inside these ranges and needn't reach their ends.
Inputs may be any that keep to these rules, and one draw needn't show every extreme that they name: `band_width`: band 0 and band 16 - 1 have width 16; widths need not grow band by band. 1 - band_width[b] <= band_start[b], so a query's own block is always seen.
All inputs are finite; a program needn't handle non-finite values.
Results may differ from the reference program's by a relative error of at most 0.006.
Values may be sent and summed in bfloat16 or wider, within the bound.
No kernel may reach another device: no remote copies, remote signals or barrier semaphores. Data moves between devices by JAX's collectives and lax.ppermute only.
A program may use at most 128 MiB of HBM per device.

```python
import jax
import jax.numpy as jnp
from jax import lax

D = 1024
HD = 64
LEV = 2
LAT_DEV = 8
LON_DEV = 16
BANDS = 16
BLOCKS = 16
NLAT = 128
NLON = 256
N_LAT = 16
N_LON = 16


def draw_q_weight(key, part):
    result = jnp.clip(jax.random.normal(jax.random.fold_in(key, 11), (D, D), jnp.float32), -6.0, 6.0) / D ** 0.5
    return result.astype(jnp.bfloat16)


def draw_k_weight(key, part):
    result = jnp.clip(jax.random.normal(jax.random.fold_in(key, 17), (D, D), jnp.float32), -6.0, 6.0) / D ** 0.5
    return result.astype(jnp.bfloat16)


def window_pattern(key):
    bands = jnp.arange(BANDS, dtype=jnp.int32)
    distance = jnp.abs(2 * bands + 1 - BANDS)
    base = 2 + distance * distance * (BLOCKS - 2) // (BANDS * BANDS)
    extra = jax.random.randint(jax.random.fold_in(key, 101), (BANDS,), 0, 2, dtype=jnp.int32)
    extra = jnp.where(bands == BANDS // 2, 0, extra)
    width = jnp.minimum(base + extra, BLOCKS)
    polar = (bands == 0) | (bands == BANDS - 1)
    width = jnp.where(polar, BLOCKS, width)
    lead = jax.random.randint(jax.random.fold_in(key, 103), (BANDS,), 0, 1048576, dtype=jnp.int32) % width
    lead = jnp.where(polar, width - 1, lead)
    return (width.astype(jnp.int32), (-lead).astype(jnp.int32))


def draw_band_width(key, part):
    return window_pattern(key)[0]


def draw_band_start(key, part):
    return window_pattern(key)[1]


def block_levels(rng, dims, split, low, largest):
    gain = 1.0
    for axis_at, shards_of in split:
        steps = jax.random.uniform(jax.random.fold_in(jax.random.fold_in(rng, 6), axis_at), (shards_of,), jnp.float32, low / len(split), largest / len(split))
        gain = gain * jnp.repeat(jnp.exp(steps), dims[axis_at] // shards_of).reshape((-1,) + (1,) * (len(dims) - 1 - axis_at))
    return gain


def normal_values(own_key, shape, deviation, most, split=(), kind=jnp.bfloat16):
    factor_of = block_levels(own_key, shape, split, -0.22, 0.18) if split else 1.0
    entries = jax.random.normal(own_key, shape, jnp.float32) * deviation * factor_of
    return jnp.minimum(jnp.maximum(entries, -most), most).astype(kind)


def setup_inputs(seed: int = 0) -> dict:
    key_of = jax.random.split(jax.random.key(seed), 9)
    tokens = normal_values(key_of[0], (NLAT, NLON, LEV, D), 1.0, 6.0, ((0, 16), (1, 16)))
    norm_gain = jnp.clip(1.0 + 0.18 * jax.random.normal(key_of[1], (D,), jnp.float32), 0.099609375, 1.8984375).astype(jnp.bfloat16)
    q_weight = draw_q_weight(jax.random.fold_in(key_of[8], 71), 0)
    k_weight = draw_k_weight(jax.random.fold_in(key_of[8], 71), 0)
    v_weight = normal_values(key_of[4], (D, D), D ** -0.5, 0.1875)
    o_weight = normal_values(key_of[5], (D, D), (D // 16) ** -0.5, 0.75)
    band_start = draw_band_start(jax.random.fold_in(key_of[8], 71), 0)
    band_width = draw_band_width(jax.random.fold_in(key_of[8], 71), 0)
    return dict(tokens=tokens, norm_gain=norm_gain, q_weight=q_weight, k_weight=k_weight, v_weight=v_weight, o_weight=o_weight, band_start=band_start, band_width=band_width)


def reference(tokens, norm_gain, q_weight, k_weight, v_weight, o_weight, band_start, band_width):
    heads = D // HD
    wide = tokens.astype(jnp.float32)
    normed = (wide * lax.rsqrt(lax.optimization_barrier(jnp.mean(wide * wide, -1, keepdims=True)) + 1e-06) * norm_gain.astype(jnp.float32)).astype(jnp.bfloat16)
    flat = normed.reshape(-1, D)
    query = jnp.dot(flat, q_weight, preferred_element_type=jnp.float32).astype(jnp.bfloat16).reshape(NLAT, NLON, LEV, D)
    keys = jnp.dot(flat, k_weight, preferred_element_type=jnp.float32).astype(jnp.bfloat16).reshape(NLAT, NLON, LEV, D)
    values = jnp.dot(flat, v_weight, preferred_element_type=jnp.float32).astype(jnp.bfloat16).reshape(NLAT, NLON, LEV, D)
    pair = jnp.stack([keys, values])
    half = NLON // 2
    top_fold = jnp.roll(pair[:, :1], -half, axis=2)
    bottom_fold = jnp.roll(pair[:, NLAT - 1:], -half, axis=2)
    extended = jnp.concatenate([top_fold, pair, bottom_fold], axis=1)
    blocks = query.reshape(N_LAT, LAT_DEV, N_LON, LON_DEV, LEV, D).transpose(0, 2, 1, 3, 4, 5)
    column_block = (jnp.arange(NLON, dtype=jnp.int32) // LON_DEV).astype(jnp.int32)
    key_block = jnp.broadcast_to(column_block[None, :, None], (LAT_DEV + 2, NLON, LEV)).reshape(-1)

    def one_band(band):
        band_pair = lax.dynamic_slice_in_dim(extended, (band * LAT_DEV).astype(jnp.int32), LAT_DEV + 2, 1)
        key_rows = band_pair[0].reshape(-1, heads, HD).astype(jnp.float32)
        value_rows = band_pair[1].reshape(-1, heads, HD).astype(jnp.float32)
        start = band_start[band]
        span = band_width[band]

        def one_block(block):
            query_rows = blocks[band, block].reshape(-1, heads, HD).astype(jnp.float32)
            seen = jnp.mod(key_block - block - start, N_LON) < span
            scores = jnp.einsum('qhd,khd->hqk', query_rows, key_rows) * HD ** (-0.5)
            scores = jnp.where(seen[None, None, :], scores, -jnp.inf)
            top = lax.optimization_barrier(jnp.max(scores, -1, keepdims=True))
            raw = jnp.exp(scores - top)
            total = lax.optimization_barrier(jnp.sum(raw, -1))
            rounded = raw.astype(jnp.bfloat16).astype(jnp.float32)
            weighted = jnp.einsum('hqk,khd->hqd', rounded, value_rows)
            result = weighted / total[..., None]
            return result.transpose(1, 0, 2).reshape(-1, D).astype(jnp.bfloat16)
        return lax.map(one_block, jnp.arange(N_LON, dtype=jnp.int32))
    attended = lax.map(one_band, jnp.arange(N_LAT, dtype=jnp.int32))
    attended = attended.reshape(N_LAT, N_LON, LAT_DEV, LON_DEV, LEV, D).transpose(0, 2, 1, 3, 4, 5).reshape(-1, D)
    mixed = wide.reshape(-1, D) + jnp.dot(attended, o_weight, preferred_element_type=jnp.float32)
    return mixed.astype(jnp.bfloat16).reshape(NLAT, NLON, LEV, D)
```

```python
import functools
import math

import jax
import jax.numpy as jnp
from jax import lax
from jax.experimental import pallas as pl
from jax.experimental.pallas import tpu as pltpu
from jax.sharding import PartitionSpec as P

HD = 64
TOK = 256
EDGE = 32
BLOCKS = 16
OWN = BLOCKS * TOK
HALO = BLOCKS * EDGE
ROWS = 80
QSCALE = HD ** -0.5 * math.log2(math.e)
SAFE = 60.0
NEG = -1e30
PAIR = 2
F32 = jnp.float32
BF16 = jnp.bfloat16
VMEM = pl.BlockSpec(memory_space=pltpu.VMEM)
SMEM = pl.BlockSpec(memory_space=pltpu.SMEM)


def project_kernel(x_ref, gain_ref, wq_ref, wk_ref, wv_ref, out_ref, normed_ref):
    @pl.when(pl.program_id(0) == 0)
    def _():
        wide = x_ref[...].astype(F32)
        mean = jnp.mean(wide * wide, -1, keepdims=True)
        normed_ref[...] = (wide * lax.rsqrt(mean + 1e-06) * gain_ref[...].astype(F32)[None, :]).astype(BF16)

    x = normed_ref[...]
    for slot, (w_ref, scale) in enumerate(((wq_ref, QSCALE), (wk_ref, None), (wv_ref, None))):
        y = jnp.dot(x, w_ref[...], preferred_element_type=F32)
        if scale is not None:
            y = y * scale
        y = y.astype(BF16).T
        for h in range(y.shape[0] // HD):
            out_ref[h, slot * HD : (slot + 1) * HD, :] = y[h * HD : (h + 1) * HD]


def project(x, gain, wq, wk, wv):
    tokens, width = x.shape
    heads = width // HD
    steps = 4
    cols = width // steps
    w_spec = pl.BlockSpec((width, cols), lambda c: (0, c))
    return pl.pallas_call(
        project_kernel,
        grid=(steps,),
        out_shape=jax.ShapeDtypeStruct((heads, 3 * HD, tokens), BF16),
        in_specs=[
            pl.BlockSpec((tokens, width), lambda c: (0, 0)),
            pl.BlockSpec((width,), lambda c: (0,)),
            w_spec,
            w_spec,
            w_spec,
        ],
        out_specs=pl.BlockSpec((heads // steps, 3 * HD, tokens), lambda c: (c, 0, 0)),
        scratch_shapes=[pltpu.VMEM((tokens, width), BF16)],
        name="project",
    )(x, gain, wq, wk, wv)


def edges_kernel(scal_ref, recv_ref, a_ref, b_ref):
    odd = scal_ref[3] == 1
    for j in range(BLOCKS):
        low = recv_ref[j, HD:, 0:128].T[:EDGE]
        high = recv_ref[j, HD:, 128:256].T[128 - EDGE :]
        rows = slice(j * EDGE, (j + 1) * EDGE)
        a_ref[rows, :] = jnp.where(odd, low, high)
        b_ref[rows, :] = jnp.where(odd, high, low)


def edges(scalars, recv):
    shape = jax.ShapeDtypeStruct((HALO, 2 * HD), BF16)
    return pl.pallas_call(
        edges_kernel,
        out_shape=(shape, shape),
        in_specs=[SMEM, VMEM],
        out_specs=[VMEM] * 2,
        compiler_params=pltpu.CompilerParams(vmem_limit_bytes=8 << 20),
        name="edges",
    )(scalars, recv)


def pieces(total, most=1536):
    spans, at = [], 0
    while at < total:
        size = min(most, total - at)
        spans.append((at, size))
        at += size
    return spans


def unit_rows():
    return (lax.broadcasted_iota(jnp.int32, (ROWS - HD, 1), 0) == 0).astype(F32)


def prepare_kernel(scal_ref, recv_ref, k_ref, vt_ref, peak_ref):
    first, final = scal_ref[0] == 0, scal_ref[0] == scal_ref[4]
    lane = lax.broadcasted_iota(jnp.int32, (1, TOK), 1)
    twice = jnp.logical_or(
        jnp.logical_and(first, lane < EDGE), jnp.logical_and(final, lane >= TOK - EDGE)
    )
    times = jnp.where(twice, 2.0, 1.0).astype(F32)
    ones = (unit_rows() * times).astype(BF16)
    q_most = jnp.zeros((1, TOK), F32)
    k_most = jnp.zeros((1, TOK), F32)
    for j in range(BLOCKS):
        q = recv_ref[j, 0:HD, :].astype(F32)
        k = recv_ref[j, HD : 2 * HD, :]
        kf = k.astype(F32)
        q_most = jnp.maximum(q_most, jnp.sum(q * q, 0, keepdims=True))
        k_most = jnp.maximum(k_most, jnp.sum(kf * kf, 0, keepdims=True))
        v = (recv_ref[j, 2 * HD :, :].astype(F32) * times).astype(BF16)
        kt = k.T
        for copy in range(2):
            at = (copy * BLOCKS + j) * TOK
            k_ref[at : at + TOK, :] = kt
            vt_ref[0:HD, at : at + TOK] = v
            vt_ref[HD:, at : at + TOK] = ones
    peak_ref[0, 0] = jnp.max(q_most)
    peak_ref[0, 1] = jnp.max(k_most)


def prepare(scalars, recv):
    return pl.pallas_call(
        prepare_kernel,
        out_shape=(
            jax.ShapeDtypeStruct((2 * OWN, HD), BF16),
            jax.ShapeDtypeStruct((ROWS, 2 * OWN), BF16),
            jax.ShapeDtypeStruct((1, 2), F32),
        ),
        in_specs=[SMEM, VMEM],
        out_specs=[VMEM, VMEM, SMEM],
        compiler_params=pltpu.CompilerParams(vmem_limit_bytes=12 << 20),
        cost_estimate=pl.CostEstimate(flops=10**9, bytes_accessed=6 << 20, transcendentals=0),
        name="prepare",
    )(scalars, recv)


def attend_kernel(scal_ref, peak_ref, recv_ref, k_ref, vt_ref, a_ref, b_ref, out_ref, hk_ref, hvt_ref):
    band, start, width = scal_ref[0], scal_ref[1], scal_ref[2]
    polar = jnp.logical_or(band == 0, band == scal_ref[4])
    k_peak = peak_ref[0, 1]
    for n, ref in enumerate((a_ref, b_ref)):
        rows = slice(n * HALO, (n + 1) * HALO)
        kv = ref[...]
        kf = kv[:, 0:HD].astype(F32)
        k_peak = jnp.maximum(k_peak, jnp.max(jnp.sum(kf * kf, 1, keepdims=True)))
        hk_ref[rows, :] = kv[:, 0:HD]
        hvt_ref[0:HD, rows] = kv.T[HD:]
        hvt_ref[HD:, rows] = jnp.broadcast_to(unit_rows(), (ROWS - HD, HALO)).astype(BF16)
    safe = peak_ref[0, 0] * k_peak < SAFE * SAFE

    def plain(acc, qt, keys, values, seen=None):
        s = jnp.dot(keys, qt, preferred_element_type=F32)
        p = jnp.exp2(s).astype(BF16)
        if seen is not None:
            values = jnp.where(seen, values.astype(F32), 0.0).astype(BF16)
        return acc + jnp.dot(values, p, preferred_element_type=F32)

    def shifted(state, qt, keys, values, seen=None):
        top, acc = state
        s = jnp.dot(keys, qt, preferred_element_type=F32)
        if seen is not None:
            s = jnp.where(seen, s, NEG)
        new = jnp.maximum(top, jnp.max(s, 0, keepdims=True))
        raw = jnp.exp2(s - new)
        if seen is not None:
            raw = jnp.where(seen, raw, 0.0)
        fresh = jnp.dot(values, raw.astype(BF16), preferred_element_type=F32)
        return new, acc * jnp.exp2(top - new) + fresh

    def own(at, size):
        return k_ref[pl.ds(at, size), :], vt_ref[:, pl.ds(at, size)]

    def halo(at, size):
        return hk_ref[pl.ds(at, size), :], hvt_ref[:, pl.ds(at, size)]

    def finish(j, acc):
        out_ref[j] = (acc[0:HD] / acc[HD : HD + 1]).astype(BF16)

    def base_of(j):
        return jnp.bitwise_and(j + start + BLOCKS, BLOCKS - 1)

    def in_window(edge_key, base):
        block = jnp.bitwise_and(lax.shift_right_logical(edge_key, 5), BLOCKS - 1)
        return jnp.bitwise_and(block - base + BLOCKS, BLOCKS - 1) < width

    zero = jnp.zeros((ROWS, TOK), F32)

    @pl.when(jnp.logical_and(safe, polar))
    def _():
        @pl.loop(0, BLOCKS, step=PAIR)
        def _(first):
            for j in (first + n for n in range(PAIR)):
                qt = recv_ref[j, 0:HD, :]
                acc = zero
                for at, size in pieces(OWN):
                    acc = plain(acc, qt, *own(at, size))
                acc = plain(acc, qt, *halo(0, HALO))
                finish(j, acc)

    grain = 4
    for count in range(grain, BLOCKS + 1, grain):
        fits = jnp.logical_and(width <= count, width > count - grain)

        @pl.when(jnp.logical_and(jnp.logical_and(safe, jnp.logical_not(polar)), fits))
        def _(count=count):
            @pl.loop(0, BLOCKS, step=PAIR)
            def _(first):
                for j in (first + n for n in range(PAIR)):
                    qt = recv_ref[j, 0:HD, :]
                    base = base_of(j)
                    acc = zero
                    for at, size in pieces(count * TOK):
                        seen = None
                        if at + size > (count - grain + 1) * TOK:
                            lanes = lax.broadcasted_iota(jnp.int32, (1, size), 1)
                            seen = lanes < width * TOK - at
                        acc = plain(acc, qt, *own(pl.multiple_of(base * TOK + at, TOK), size), seen)
                    lanes = lax.broadcasted_iota(jnp.int32, (1, 2 * HALO), 1)
                    acc = plain(acc, qt, *halo(0, 2 * HALO), in_window(lanes, base))
                    finish(j, acc)

    @pl.when(jnp.logical_not(safe))
    def _():
        @pl.loop(0, BLOCKS)
        def _(j):
            qt = recv_ref[j, 0:HD, :]
            base = base_of(j)

            def own_step(n, state):
                return shifted(state, qt, *own(pl.multiple_of((base + n) * TOK, TOK), TOK))

            def halo_step(n, state):
                at = pl.multiple_of(n * TOK, TOK)
                row = lax.broadcasted_iota(jnp.int32, (TOK, 1), 0) + at
                return shifted(state, qt, *halo(at, TOK), in_window(row, base))

            state = (jnp.full((1, TOK), NEG, F32), zero)
            state = lax.fori_loop(0, width, own_step, state)
            sides = jnp.where(polar, HALO // TOK, 2 * HALO // TOK)
            state = lax.fori_loop(0, sides, halo_step, state)
            finish(j, state[1])


def attend(scalars, peaks, recv, keys, values, side_a, side_b):
    return pl.pallas_call(
        attend_kernel,
        out_shape=jax.ShapeDtypeStruct((BLOCKS, HD, TOK), BF16),
        in_specs=[SMEM, SMEM] + [VMEM] * 5,
        out_specs=VMEM,
        scratch_shapes=[
            pltpu.VMEM((2 * HALO, HD), BF16),
            pltpu.VMEM((ROWS, 2 * HALO), BF16),
        ],
        compiler_params=pltpu.CompilerParams(vmem_limit_bytes=24 << 20),
        cost_estimate=pl.CostEstimate(
            flops=4 * OWN * OWN * HD, bytes_accessed=8 << 20, transcendentals=OWN * OWN
        ),
        name="attend",
    )(scalars, peaks, recv, keys, values, side_a, side_b)


def mix_kernel(att_ref, wo_ref, x_ref, out_ref, rows_ref):
    @pl.when(pl.program_id(0) == 0)
    def _():
        rows_ref[...] = att_ref[...].T

    y = jnp.dot(rows_ref[...], wo_ref[...], preferred_element_type=F32)
    out_ref[...] = (x_ref[...].astype(F32) + y).astype(BF16)


def mix(att, wo, x):
    tokens, width = x.shape
    steps = 4
    cols = width // steps
    return pl.pallas_call(
        mix_kernel,
        grid=(steps,),
        out_shape=jax.ShapeDtypeStruct((tokens, width), BF16),
        in_specs=[
            pl.BlockSpec((width, tokens), lambda c: (0, 0)),
            pl.BlockSpec((width, cols), lambda c: (0, c)),
            pl.BlockSpec((tokens, cols), lambda c: (0, c)),
        ],
        out_specs=pl.BlockSpec((tokens, cols), lambda c: (0, c)),
        scratch_shapes=[pltpu.VMEM((tokens, width), BF16)],
        name="mix",
    )(att, wo, x)


def swap(value):
    return lax.all_to_all(value, "lon", split_axis=0, concat_axis=0, tiled=True)


def body(tokens, norm_gain, q_weight, k_weight, v_weight, o_weight, band_start, band_width):
    width = tokens.shape[-1]
    n_lat = lax.axis_size("lat")
    band = lax.axis_index("lat")
    scalars = jnp.stack(
        [band, band_start[band], band_width[band], jnp.bitwise_and(band, 1), jnp.int32(n_lat - 1)]
    )
    x = tokens.reshape(-1, width)
    recv = swap(project(x, norm_gain, q_weight, k_weight, v_weight))
    side_a, side_b = edges(scalars, recv)
    pairs_a = [(b, b ^ 1) for b in range(n_lat)]
    pairs_b = [(b, ((b - 1) ^ 1) + 1) for b in range(1, n_lat - 1)]
    side_a = lax.ppermute(side_a, "lat", pairs_a)
    side_b = lax.ppermute(side_b, "lat", pairs_b)
    keys, values, peaks = prepare(scalars, recv)
    att = swap(attend(scalars, peaks, recv, keys, values, side_a, side_b))
    mixed = mix(att.reshape(width, -1), o_weight, x)
    return mixed.reshape(tokens.shape)


def solution(mesh):
    placed = (P("lat", "lon", None, None), P(), P(), P(), P(), P(), P(), P())
    return jax.shard_map(
        body, mesh=mesh, in_specs=placed, out_specs=P("lat", "lon", None, None), check_vma=False
    )
```

```python
import functools
import math

import jax
import jax.numpy as jnp
from jax import lax
from jax.experimental import pallas as pl
from jax.experimental.pallas import tpu as pltpu
from jax.sharding import PartitionSpec as P

HD = 64
TOK = 256
EDGE = 32
BLOCKS = 16
OWN = BLOCKS * TOK
HALO = BLOCKS * EDGE
ROWS = 80
QSCALE = HD ** -0.5 * math.log2(math.e)
SAFE = 60.0
NEG = -1e30
PAIR = 2
F32 = jnp.float32
BF16 = jnp.bfloat16
VMEM = pl.BlockSpec(memory_space=pltpu.VMEM)
SMEM = pl.BlockSpec(memory_space=pltpu.SMEM)


def project_kernel(x_ref, gain_ref, wq_ref, wk_ref, wv_ref, out_ref, normed_ref):
    @pl.when(pl.program_id(0) == 0)
    def _():
        wide = x_ref[...].reshape(normed_ref.shape).astype(F32)
        mean = jnp.mean(wide * wide, -1, keepdims=True)
        normed_ref[...] = (wide * lax.rsqrt(mean + 1e-06) * gain_ref[...].astype(F32)[None, :]).astype(BF16)

    x = normed_ref[...]
    for slot, (w_ref, scale) in enumerate(((wq_ref, QSCALE), (wk_ref, None), (wv_ref, None))):
        y = jnp.dot(x, w_ref[...], preferred_element_type=F32)
        if scale is not None:
            y = y * scale
        y = y.astype(BF16).T
        for h in range(y.shape[0] // HD):
            out_ref[h, slot * HD : (slot + 1) * HD, :] = y[h * HD : (h + 1) * HD]


def project(x, gain, wq, wk, wv):
    width = x.shape[-1]
    tokens = x.size // width
    heads = width // HD
    steps = 2
    cols = width // steps
    w_spec = pl.BlockSpec((width, cols), lambda c: (0, c))
    return pl.pallas_call(
        project_kernel,
        grid=(steps,),
        out_shape=jax.ShapeDtypeStruct((heads, 3 * HD, tokens), BF16),
        in_specs=[
            pl.BlockSpec(x.shape, lambda c: (0, 0, 0, 0)),
            pl.BlockSpec((width,), lambda c: (0,)),
            w_spec,
            w_spec,
            w_spec,
        ],
        out_specs=pl.BlockSpec((heads // steps, 3 * HD, tokens), lambda c: (c, 0, 0)),
        scratch_shapes=[pltpu.VMEM((tokens, width), BF16)],
        name="project",
    )(x, gain, wq, wk, wv)


def edges_kernel(scal_ref, recv_ref, a_ref, b_ref):
    odd = scal_ref[3] == 1
    for j in range(BLOCKS):
        low = recv_ref[j, HD:, 0:128].T[:EDGE]
        high = recv_ref[j, HD:, 128:256].T[128 - EDGE :]
        rows = slice(j * EDGE, (j + 1) * EDGE)
        a_ref[rows, :] = jnp.where(odd, low, high)
        b_ref[rows, :] = jnp.where(odd, high, low)


def edges(scalars, recv):
    shape = jax.ShapeDtypeStruct((HALO, 2 * HD), BF16)
    return pl.pallas_call(
        edges_kernel,
        out_shape=(shape, shape),
        in_specs=[SMEM, VMEM],
        out_specs=[VMEM] * 2,
        compiler_params=pltpu.CompilerParams(vmem_limit_bytes=8 << 20),
        name="edges",
    )(scalars, recv)


def pieces(total, most=1536):
    spans, at = [], 0
    while at < total:
        size = min(most, total - at)
        spans.append((at, size))
        at += size
    return spans


def unit_rows():
    return (lax.broadcasted_iota(jnp.int32, (ROWS - HD, 1), 0) == 0).astype(F32)


def prepare_kernel(scal_ref, recv_ref, k_ref, vt_ref, peak_ref):
    first, final = scal_ref[0] == 0, scal_ref[0] == scal_ref[4]
    lane = lax.broadcasted_iota(jnp.int32, (1, TOK), 1)
    twice = jnp.logical_or(
        jnp.logical_and(first, lane < EDGE), jnp.logical_and(final, lane >= TOK - EDGE)
    )
    times = jnp.where(twice, 2.0, 1.0).astype(F32)
    ones = (unit_rows() * times).astype(BF16)
    q_most = jnp.zeros((1, TOK), F32)
    k_most = jnp.zeros((1, TOK), F32)
    for j in range(BLOCKS):
        q = recv_ref[j, 0:HD, :].astype(F32)
        k = recv_ref[j, HD : 2 * HD, :]
        kf = k.astype(F32)
        q_most = jnp.maximum(q_most, jnp.sum(q * q, 0, keepdims=True))
        k_most = jnp.maximum(k_most, jnp.sum(kf * kf, 0, keepdims=True))
        v = (recv_ref[j, 2 * HD :, :].astype(F32) * times).astype(BF16)
        kt = k.T
        for copy in range(2):
            at = (copy * BLOCKS + j) * TOK
            k_ref[at : at + TOK, :] = kt
            vt_ref[0:HD, at : at + TOK] = v
            vt_ref[HD:, at : at + TOK] = ones
    peak_ref[0, 0] = jnp.max(q_most)
    peak_ref[0, 1] = jnp.max(k_most)


def prepare(scalars, recv):
    return pl.pallas_call(
        prepare_kernel,
        out_shape=(
            jax.ShapeDtypeStruct((2 * OWN, HD), BF16),
            jax.ShapeDtypeStruct((ROWS, 2 * OWN), BF16),
            jax.ShapeDtypeStruct((1, 2), F32),
        ),
        in_specs=[SMEM, VMEM],
        out_specs=[VMEM, VMEM, SMEM],
        compiler_params=pltpu.CompilerParams(vmem_limit_bytes=12 << 20),
        cost_estimate=pl.CostEstimate(flops=10**9, bytes_accessed=6 << 20, transcendentals=0),
        name="prepare",
    )(scalars, recv)


def attend_kernel(scal_ref, peak_ref, recv_ref, k_ref, vt_ref, a_ref, b_ref, out_ref, hk_ref, hvt_ref):
    band, start, width = scal_ref[0], scal_ref[1], scal_ref[2]
    polar = jnp.logical_or(band == 0, band == scal_ref[4])
    k_peak = peak_ref[0, 1]
    for n, ref in enumerate((a_ref, b_ref)):
        rows = slice(n * HALO, (n + 1) * HALO)
        kv = ref[...]
        kf = kv[:, 0:HD].astype(F32)
        k_peak = jnp.maximum(k_peak, jnp.max(jnp.sum(kf * kf, 1, keepdims=True)))
        hk_ref[rows, :] = kv[:, 0:HD]
        hvt_ref[0:HD, rows] = kv.T[HD:]
        hvt_ref[HD:, rows] = jnp.broadcast_to(unit_rows(), (ROWS - HD, HALO)).astype(BF16)
    safe = peak_ref[0, 0] * k_peak < SAFE * SAFE

    def plain(acc, qt, keys, values, seen=None):
        s = jnp.dot(keys, qt, preferred_element_type=F32)
        p = jnp.exp2(s).astype(BF16)
        if seen is not None:
            values = jnp.where(seen, values.astype(F32), 0.0).astype(BF16)
        return acc + jnp.dot(values, p, preferred_element_type=F32)

    def shifted(state, qt, keys, values, seen=None):
        top, acc = state
        s = jnp.dot(keys, qt, preferred_element_type=F32)
        if seen is not None:
            s = jnp.where(seen, s, NEG)
        new = jnp.maximum(top, jnp.max(s, 0, keepdims=True))
        raw = jnp.exp2(s - new)
        if seen is not None:
            raw = jnp.where(seen, raw, 0.0)
        fresh = jnp.dot(values, raw.astype(BF16), preferred_element_type=F32)
        return new, acc * jnp.exp2(top - new) + fresh

    def own(at, size):
        return k_ref[pl.ds(at, size), :], vt_ref[:, pl.ds(at, size)]

    def halo(at, size):
        return hk_ref[pl.ds(at, size), :], hvt_ref[:, pl.ds(at, size)]

    def finish(j, acc):
        out_ref[j] = (acc[0:HD] / acc[HD : HD + 1]).astype(BF16)

    def base_of(j):
        return jnp.bitwise_and(j + start + BLOCKS, BLOCKS - 1)

    def in_window(edge_key, base):
        block = jnp.bitwise_and(lax.shift_right_logical(edge_key, 5), BLOCKS - 1)
        return jnp.bitwise_and(block - base + BLOCKS, BLOCKS - 1) < width

    zero = jnp.zeros((ROWS, TOK), F32)

    @pl.when(jnp.logical_and(safe, polar))
    def _():
        @pl.loop(0, BLOCKS, step=PAIR)
        def _(first):
            for j in (first + n for n in range(PAIR)):
                qt = recv_ref[j, 0:HD, :]
                acc = zero
                for at, size in pieces(OWN):
                    acc = plain(acc, qt, *own(at, size))
                acc = plain(acc, qt, *halo(0, HALO))
                finish(j, acc)

    grain = 4
    for count in range(grain, BLOCKS + 1, grain):
        fits = jnp.logical_and(width <= count, width > count - grain)

        @pl.when(jnp.logical_and(jnp.logical_and(safe, jnp.logical_not(polar)), fits))
        def _(count=count):
            @pl.loop(0, BLOCKS, step=PAIR)
            def _(first):
                for j in (first + n for n in range(PAIR)):
                    qt = recv_ref[j, 0:HD, :]
                    base = base_of(j)
                    acc = zero
                    for at, size in pieces(count * TOK):
                        seen = None
                        if at + size > (count - grain + 1) * TOK:
                            lanes = lax.broadcasted_iota(jnp.int32, (1, size), 1)
                            seen = lanes < width * TOK - at
                        acc = plain(acc, qt, *own(pl.multiple_of(base * TOK + at, TOK), size), seen)
                    lanes = lax.broadcasted_iota(jnp.int32, (1, 2 * HALO), 1)
                    acc = plain(acc, qt, *halo(0, 2 * HALO), in_window(lanes, base))
                    finish(j, acc)

    @pl.when(jnp.logical_not(safe))
    def _():
        @pl.loop(0, BLOCKS)
        def _(j):
            qt = recv_ref[j, 0:HD, :]
            base = base_of(j)

            def own_step(n, state):
                return shifted(state, qt, *own(pl.multiple_of((base + n) * TOK, TOK), TOK))

            def halo_step(n, state):
                at = pl.multiple_of(n * TOK, TOK)
                row = lax.broadcasted_iota(jnp.int32, (TOK, 1), 0) + at
                return shifted(state, qt, *halo(at, TOK), in_window(row, base))

            state = (jnp.full((1, TOK), NEG, F32), zero)
            state = lax.fori_loop(0, width, own_step, state)
            sides = jnp.where(polar, HALO // TOK, 2 * HALO // TOK)
            state = lax.fori_loop(0, sides, halo_step, state)
            finish(j, state[1])


def attend(scalars, peaks, recv, keys, values, side_a, side_b):
    return pl.pallas_call(
        attend_kernel,
        out_shape=jax.ShapeDtypeStruct((BLOCKS, HD, TOK), BF16),
        in_specs=[SMEM, SMEM] + [VMEM] * 5,
        out_specs=VMEM,
        scratch_shapes=[
            pltpu.VMEM((2 * HALO, HD), BF16),
            pltpu.VMEM((ROWS, 2 * HALO), BF16),
        ],
        compiler_params=pltpu.CompilerParams(vmem_limit_bytes=24 << 20),
        cost_estimate=pl.CostEstimate(
            flops=4 * OWN * OWN * HD, bytes_accessed=8 << 20, transcendentals=OWN * OWN
        ),
        name="attend",
    )(scalars, peaks, recv, keys, values, side_a, side_b)


def mix_kernel(att_ref, wo_ref, x_ref, out_ref):
    rows = att_ref[...].T
    width = wo_ref.shape[1]
    cols = width // 2
    for at in range(0, width, cols):
        part = slice(at, at + cols)
        y = jnp.dot(rows, wo_ref[:, part], preferred_element_type=F32)
        y = y + x_ref[:, :, :, part].reshape(y.shape).astype(F32)
        out_ref[:, :, :, part] = y.astype(BF16).reshape(out_ref.shape[:3] + (cols,))


def mix(att, wo, x):
    return pl.pallas_call(
        mix_kernel,
        out_shape=jax.ShapeDtypeStruct(x.shape, BF16),
        in_specs=[VMEM] * 3,
        out_specs=VMEM,
        compiler_params=pltpu.CompilerParams(vmem_limit_bytes=10 << 20),
        name="mix",
    )(att, wo, x)


def swap(value):
    return lax.all_to_all(value, "lon", split_axis=0, concat_axis=0, tiled=True)


def body(tokens, norm_gain, q_weight, k_weight, v_weight, o_weight, band_start, band_width):
    width = tokens.shape[-1]
    n_lat = lax.axis_size("lat")
    band = lax.axis_index("lat")
    scalars = jnp.stack(
        [band, band_start[band], band_width[band], jnp.bitwise_and(band, 1), jnp.int32(n_lat - 1)]
    )
    recv = swap(project(tokens, norm_gain, q_weight, k_weight, v_weight))
    side_a, side_b = edges(scalars, recv)
    pairs_a = [(b, b ^ 1) for b in range(n_lat)]
    pairs_b = [(b, ((b - 1) ^ 1) + 1) for b in range(1, n_lat - 1)]
    side_a = lax.ppermute(side_a, "lat", pairs_a)
    side_b = lax.ppermute(side_b, "lat", pairs_b)
    keys, values, peaks = prepare(scalars, recv)
    att = swap(attend(scalars, peaks, recv, keys, values, side_a, side_b))
    return mix(att.reshape(width, -1), o_weight, tokens)


def solution(mesh):
    placed = (P("lat", "lon", None, None), P(), P(), P(), P(), P(), P(), P())
    return jax.shard_map(
        body, mesh=mesh, in_specs=placed, out_specs=P("lat", "lon", None, None), check_vma=False
    )
```

```python
import functools
import math

import jax
import jax.numpy as jnp
from jax import lax
from jax.experimental import pallas as pl
from jax.experimental.pallas import tpu as pltpu
from jax.sharding import PartitionSpec as P

HD = 64
TOK = 256
EDGE = 32
BLOCKS = 16
OWN = BLOCKS * TOK
HALO = BLOCKS * EDGE
ROWS = 80
QSCALE = HD ** -0.5 * math.log2(math.e)
SAFE = 60.0
NEG = -1e30
PAIR = 2
PRE = 2
GRAIN = 4
F32 = jnp.float32
BF16 = jnp.bfloat16
VMEM = pl.BlockSpec(memory_space=pltpu.VMEM)
SMEM = pl.BlockSpec(memory_space=pltpu.SMEM)


def project_kernel(x_ref, gain_ref, wq_ref, wk_ref, wv_ref, out_ref, normed_ref):
    @pl.when(pl.program_id(0) == 0)
    def _():
        wide = x_ref[...].reshape(normed_ref.shape).astype(F32)
        mean = jnp.mean(wide * wide, -1, keepdims=True)
        normed_ref[...] = (wide * lax.rsqrt(mean + 1e-06) * gain_ref[...].astype(F32)[None, :]).astype(BF16)

    x = normed_ref[...]
    for slot, (w_ref, scale) in enumerate(((wq_ref, QSCALE), (wk_ref, None), (wv_ref, None))):
        y = jnp.dot(x, w_ref[...], preferred_element_type=F32)
        if scale is not None:
            y = y * scale
        y = y.astype(BF16).T
        for h in range(y.shape[0] // HD):
            out_ref[h, slot * HD : (slot + 1) * HD, :] = y[h * HD : (h + 1) * HD]


def project(x, gain, wq, wk, wv):
    width = x.shape[-1]
    tokens = x.size // width
    heads = width // HD
    steps = 2
    cols = width // steps
    w_spec = pl.BlockSpec((width, cols), lambda c: (0, c))
    return pl.pallas_call(
        project_kernel,
        grid=(steps,),
        out_shape=jax.ShapeDtypeStruct((heads, 3 * HD, tokens), BF16),
        in_specs=[
            pl.BlockSpec(x.shape, lambda c: (0, 0, 0, 0)),
            pl.BlockSpec((width,), lambda c: (0,)),
            w_spec,
            w_spec,
            w_spec,
        ],
        out_specs=pl.BlockSpec((heads // steps, 3 * HD, tokens), lambda c: (c, 0, 0)),
        scratch_shapes=[pltpu.VMEM((tokens, width), BF16)],
        name="project",
    )(x, gain, wq, wk, wv)


def edges_kernel(scal_ref, recv_ref, a_ref, b_ref):
    odd = scal_ref[3] == 1
    for j in range(BLOCKS):
        low = recv_ref[j, HD:, 0:128].T[:EDGE]
        high = recv_ref[j, HD:, 128:256].T[128 - EDGE :]
        rows = slice(j * EDGE, (j + 1) * EDGE)
        a_ref[rows, :] = jnp.where(odd, low, high)
        b_ref[rows, :] = jnp.where(odd, high, low)


def edges(scalars, recv):
    shape = jax.ShapeDtypeStruct((HALO, 2 * HD), BF16)
    return pl.pallas_call(
        edges_kernel,
        out_shape=(shape, shape),
        in_specs=[SMEM, VMEM],
        out_specs=[VMEM] * 2,
        compiler_params=pltpu.CompilerParams(vmem_limit_bytes=8 << 20),
        name="edges",
    )(scalars, recv)


def pieces(total, most=1536):
    spans, at = [], 0
    while at < total:
        size = min(most, total - at)
        spans.append((at, size))
        at += size
    return spans


def variants(width, polar):
    yield None, polar
    for count in range(GRAIN, BLOCKS + 1, GRAIN):
        fits = jnp.logical_and(width <= count, width > count - GRAIN)
        yield count, jnp.logical_and(jnp.logical_not(polar), fits)


def unit_rows():
    return (lax.broadcasted_iota(jnp.int32, (ROWS - HD, 1), 0) == 0).astype(F32)


def plain(acc, qt, keys, values, seen=None):
    s = jnp.dot(keys, qt, preferred_element_type=F32)
    p = jnp.exp2(s).astype(BF16)
    if seen is not None:
        values = jnp.where(seen, values.astype(F32), 0.0).astype(BF16)
    return acc + jnp.dot(values, p, preferred_element_type=F32)


def window_base(j, start):
    return jnp.bitwise_and(j + start + BLOCKS, BLOCKS - 1)


def own_part(qt, base, width, count, k_ref, vt_ref):
    acc = jnp.zeros((ROWS, TOK), F32)
    for at, size in pieces(count * TOK):
        if base is None:
            place, seen = at, None
        else:
            place = pl.multiple_of(base * TOK + at, TOK)
            seen = None
            if at + size > (count - GRAIN + 1) * TOK:
                seen = lax.broadcasted_iota(jnp.int32, (1, size), 1) < width * TOK - at
        acc = plain(acc, qt, k_ref[pl.ds(place, size), :], vt_ref[:, pl.ds(place, size)], seen)
    return acc


def prepare_kernel(scal_ref, recv_ref, k_ref, vt_ref, peak_ref, acc_ref):
    start, width = scal_ref[1], scal_ref[2]
    first, final = scal_ref[0] == 0, scal_ref[0] == scal_ref[4]
    lane = lax.broadcasted_iota(jnp.int32, (1, TOK), 1)
    twice = jnp.logical_or(
        jnp.logical_and(first, lane < EDGE), jnp.logical_and(final, lane >= TOK - EDGE)
    )
    times = jnp.where(twice, 2.0, 1.0).astype(F32)
    ones = (unit_rows() * times).astype(BF16)
    q_most = jnp.zeros((1, TOK), F32)
    k_most = jnp.zeros((1, TOK), F32)
    for j in range(BLOCKS):
        q = recv_ref[j, 0:HD, :].astype(F32)
        k = recv_ref[j, HD : 2 * HD, :]
        kf = k.astype(F32)
        q_most = jnp.maximum(q_most, jnp.sum(q * q, 0, keepdims=True))
        k_most = jnp.maximum(k_most, jnp.sum(kf * kf, 0, keepdims=True))
        v = (recv_ref[j, 2 * HD :, :].astype(F32) * times).astype(BF16)
        kt = k.T
        for copy in range(2):
            at = (copy * BLOCKS + j) * TOK
            k_ref[at : at + TOK, :] = kt
            vt_ref[0:HD, at : at + TOK] = v
            vt_ref[HD:, at : at + TOK] = ones
    q_peak = jnp.max(q_most)
    k_peak = jnp.max(k_most)
    peak_ref[0, 0] = q_peak
    peak_ref[0, 1] = k_peak
    safe = q_peak * k_peak < SAFE * SAFE
    for count, fits in variants(width, jnp.logical_or(first, final)):

        @pl.when(jnp.logical_and(safe, fits))
        def _(count=count):
            for j in range(PRE):
                base = None if count is None else window_base(j, start)
                qt = recv_ref[j, 0:HD, :]
                acc_ref[j] = own_part(qt, base, width, count or BLOCKS, k_ref, vt_ref)


def prepare(scalars, recv):
    return pl.pallas_call(
        prepare_kernel,
        out_shape=(
            jax.ShapeDtypeStruct((2 * OWN, HD), BF16),
            jax.ShapeDtypeStruct((ROWS, 2 * OWN), BF16),
            jax.ShapeDtypeStruct((1, 2), F32),
            jax.ShapeDtypeStruct((PRE, ROWS, TOK), F32),
        ),
        in_specs=[SMEM, VMEM],
        out_specs=[VMEM, VMEM, SMEM, VMEM],
        compiler_params=pltpu.CompilerParams(vmem_limit_bytes=16 << 20),
        cost_estimate=pl.CostEstimate(flops=10**9, bytes_accessed=6 << 20, transcendentals=0),
        name="prepare",
    )(scalars, recv)


def attend_kernel(scal_ref, peak_ref, recv_ref, k_ref, vt_ref, pre_ref, a_ref, b_ref, out_ref, hk_ref, hvt_ref):
    band, start, width = scal_ref[0], scal_ref[1], scal_ref[2]
    polar = jnp.logical_or(band == 0, band == scal_ref[4])
    k_peak = peak_ref[0, 1]
    for n, ref in enumerate((a_ref, b_ref)):
        rows = slice(n * HALO, (n + 1) * HALO)
        kv = ref[...]
        kf = kv[:, 0:HD].astype(F32)
        k_peak = jnp.maximum(k_peak, jnp.max(jnp.sum(kf * kf, 1, keepdims=True)))
        hk_ref[rows, :] = kv[:, 0:HD]
        hvt_ref[0:HD, rows] = kv.T[HD:]
        hvt_ref[HD:, rows] = jnp.broadcast_to(unit_rows(), (ROWS - HD, HALO)).astype(BF16)
    safe = peak_ref[0, 0] * k_peak < SAFE * SAFE

    def shifted(state, qt, keys, values, seen=None):
        top, acc = state
        s = jnp.dot(keys, qt, preferred_element_type=F32)
        if seen is not None:
            s = jnp.where(seen, s, NEG)
        new = jnp.maximum(top, jnp.max(s, 0, keepdims=True))
        raw = jnp.exp2(s - new)
        if seen is not None:
            raw = jnp.where(seen, raw, 0.0)
        fresh = jnp.dot(values, raw.astype(BF16), preferred_element_type=F32)
        return new, acc * jnp.exp2(top - new) + fresh

    def own(at, size):
        return k_ref[pl.ds(at, size), :], vt_ref[:, pl.ds(at, size)]

    def halo(at, size):
        return hk_ref[pl.ds(at, size), :], hvt_ref[:, pl.ds(at, size)]

    def finish(j, acc):
        out_ref[j] = (acc[0:HD] / acc[HD : HD + 1]).astype(BF16)

    def in_window(edge_key, base):
        block = jnp.bitwise_and(lax.shift_right_logical(edge_key, 5), BLOCKS - 1)
        return jnp.bitwise_and(block - base + BLOCKS, BLOCKS - 1) < width

    def add_halo(j, acc, one_side):
        qt = recv_ref[j, 0:HD, :]
        if one_side:
            acc = plain(acc, qt, *halo(0, HALO))
        else:
            lanes = lax.broadcasted_iota(jnp.int32, (1, 2 * HALO), 1)
            acc = plain(acc, qt, *halo(0, 2 * HALO), in_window(lanes, window_base(j, start)))
        finish(j, acc)

    for one_side, here in ((True, polar), (False, jnp.logical_not(polar))):

        @pl.when(jnp.logical_and(safe, here))
        def _(one_side=one_side):
            for j in range(PRE):
                add_halo(j, pre_ref[j], one_side)

    for count, fits in variants(width, polar):

        @pl.when(jnp.logical_and(safe, fits))
        def _(count=count):
            @pl.loop(PRE, BLOCKS, step=PAIR)
            def _(first):
                for j in (first + n for n in range(PAIR)):
                    base = None if count is None else window_base(j, start)
                    qt = recv_ref[j, 0:HD, :]
                    acc = own_part(qt, base, width, count or BLOCKS, k_ref, vt_ref)
                    add_halo(j, acc, count is None)

    @pl.when(jnp.logical_not(safe))
    def _():
        @pl.loop(0, BLOCKS)
        def _(j):
            qt = recv_ref[j, 0:HD, :]
            base = window_base(j, start)

            def own_step(n, state):
                return shifted(state, qt, *own(pl.multiple_of((base + n) * TOK, TOK), TOK))

            def halo_step(n, state):
                at = pl.multiple_of(n * TOK, TOK)
                row = lax.broadcasted_iota(jnp.int32, (TOK, 1), 0) + at
                return shifted(state, qt, *halo(at, TOK), in_window(row, base))

            state = (jnp.full((1, TOK), NEG, F32), jnp.zeros((ROWS, TOK), F32))
            state = lax.fori_loop(0, width, own_step, state)
            sides = jnp.where(polar, HALO // TOK, 2 * HALO // TOK)
            state = lax.fori_loop(0, sides, halo_step, state)
            finish(j, state[1])


def attend(scalars, peaks, recv, keys, values, pre, side_a, side_b):
    return pl.pallas_call(
        attend_kernel,
        out_shape=jax.ShapeDtypeStruct((BLOCKS, HD, TOK), BF16),
        in_specs=[SMEM, SMEM] + [VMEM] * 6,
        out_specs=VMEM,
        scratch_shapes=[
            pltpu.VMEM((2 * HALO, HD), BF16),
            pltpu.VMEM((ROWS, 2 * HALO), BF16),
        ],
        compiler_params=pltpu.CompilerParams(vmem_limit_bytes=24 << 20),
        cost_estimate=pl.CostEstimate(
            flops=4 * OWN * OWN * HD, bytes_accessed=8 << 20, transcendentals=OWN * OWN
        ),
        name="attend",
    )(scalars, peaks, recv, keys, values, pre, side_a, side_b)


def mix_kernel(att_ref, wo_ref, x_ref, out_ref):
    rows = att_ref[...].T
    width = wo_ref.shape[1]
    cols = width // 2
    for at in range(0, width, cols):
        part = slice(at, at + cols)
        y = jnp.dot(rows, wo_ref[:, part], preferred_element_type=F32)
        y = y + x_ref[:, :, :, part].reshape(y.shape).astype(F32)
        out_ref[:, :, :, part] = y.astype(BF16).reshape(out_ref.shape[:3] + (cols,))


def mix(att, wo, x):
    return pl.pallas_call(
        mix_kernel,
        out_shape=jax.ShapeDtypeStruct(x.shape, BF16),
        in_specs=[VMEM] * 3,
        out_specs=VMEM,
        compiler_params=pltpu.CompilerParams(vmem_limit_bytes=10 << 20),
        name="mix",
    )(att, wo, x)


def swap(value):
    return lax.all_to_all(value, "lon", split_axis=0, concat_axis=0, tiled=True)


def body(tokens, norm_gain, q_weight, k_weight, v_weight, o_weight, band_start, band_width):
    width = tokens.shape[-1]
    n_lat = lax.axis_size("lat")
    band = lax.axis_index("lat")
    scalars = jnp.stack(
        [band, band_start[band], band_width[band], jnp.bitwise_and(band, 1), jnp.int32(n_lat - 1)]
    )
    recv = swap(project(tokens, norm_gain, q_weight, k_weight, v_weight))
    side_a, side_b = edges(scalars, recv)
    pairs_a = [(b, b ^ 1) for b in range(n_lat)]
    pairs_b = [(b, ((b - 1) ^ 1) + 1) for b in range(1, n_lat - 1)]
    side_a = lax.ppermute(side_a, "lat", pairs_a)
    side_b = lax.ppermute(side_b, "lat", pairs_b)
    keys, values, peaks, pre = prepare(scalars, recv)
    att = swap(attend(scalars, peaks, recv, keys, values, pre, side_a, side_b))
    return mix(att.reshape(width, -1), o_weight, tokens)


def solution(mesh):
    placed = (P("lat", "lon", None, None), P(), P(), P(), P(), P(), P(), P())
    return jax.shard_map(
        body, mesh=mesh, in_specs=placed, out_specs=P("lat", "lon", None, None), check_vma=False
    )
```

```python
import functools
import math

import jax
import jax.numpy as jnp
from jax import lax
from jax.experimental import pallas as pl
from jax.experimental.pallas import tpu as pltpu
from jax.sharding import PartitionSpec as P

HD = 64
TOK = 256
EDGE = 32
BLOCKS = 16
OWN = BLOCKS * TOK
HALO = BLOCKS * EDGE
ROWS = 80
QSCALE = HD ** -0.5 * math.log2(math.e)
SAFE = 60.0
NEG = -1e30
PAIR = 2
PRE = 2
GRAIN = 4
F32 = jnp.float32
BF16 = jnp.bfloat16
VMEM = pl.BlockSpec(memory_space=pltpu.VMEM)
SMEM = pl.BlockSpec(memory_space=pltpu.SMEM)


def project_kernel(x_ref, gain_ref, wq_ref, wk_ref, wv_ref, out_ref, normed_ref):
    @pl.when(pl.program_id(0) == 0)
    def _():
        wide = x_ref[...].reshape(normed_ref.shape).astype(F32)
        mean = jnp.mean(wide * wide, -1, keepdims=True)
        normed_ref[...] = (wide * lax.rsqrt(mean + 1e-06) * gain_ref[...].astype(F32)[None, :]).astype(BF16)

    x = normed_ref[...]
    for slot, (w_ref, scale) in enumerate(((wq_ref, QSCALE), (wk_ref, None), (wv_ref, None))):
        y = jnp.dot(x, w_ref[...], preferred_element_type=F32)
        if scale is not None:
            y = y * scale
        y = y.astype(BF16).T
        for h in range(y.shape[0] // HD):
            out_ref[h, slot * HD : (slot + 1) * HD, :] = y[h * HD : (h + 1) * HD]


def project(x, gain, wq, wk, wv):
    width = x.shape[-1]
    tokens = x.size // width
    heads = width // HD
    steps = 2
    cols = width // steps
    w_spec = pl.BlockSpec((width, cols), lambda c: (0, c))
    return pl.pallas_call(
        project_kernel,
        grid=(steps,),
        out_shape=jax.ShapeDtypeStruct((heads, 3 * HD, tokens), BF16),
        in_specs=[
            pl.BlockSpec(x.shape, lambda c: (0, 0, 0, 0)),
            pl.BlockSpec((width,), lambda c: (0,)),
            w_spec,
            w_spec,
            w_spec,
        ],
        out_specs=pl.BlockSpec((heads // steps, 3 * HD, tokens), lambda c: (c, 0, 0)),
        scratch_shapes=[pltpu.VMEM((tokens, width), BF16)],
        name="project",
    )(x, gain, wq, wk, wv)


def edges_kernel(scal_ref, recv_ref, a_ref, b_ref):
    odd = scal_ref[3] == 1
    for j in range(BLOCKS):
        low = recv_ref[j, HD:, 0:128].T[:EDGE]
        high = recv_ref[j, HD:, 128:256].T[128 - EDGE :]
        rows = slice(j * EDGE, (j + 1) * EDGE)
        a_ref[rows, :] = jnp.where(odd, low, high)
        b_ref[rows, :] = jnp.where(odd, high, low)


def edges(scalars, recv):
    shape = jax.ShapeDtypeStruct((HALO, 2 * HD), BF16)
    return pl.pallas_call(
        edges_kernel,
        out_shape=(shape, shape),
        in_specs=[SMEM, VMEM],
        out_specs=[VMEM] * 2,
        compiler_params=pltpu.CompilerParams(vmem_limit_bytes=8 << 20),
        name="edges",
    )(scalars, recv)


def pieces(total, most=1536):
    spans, at = [], 0
    while at < total:
        size = min(most, total - at)
        spans.append((at, size))
        at += size
    return spans


def variants(width, polar):
    yield None, polar
    for count in range(GRAIN, BLOCKS + 1, GRAIN):
        fits = jnp.logical_and(width <= count, width > count - GRAIN)
        yield count, jnp.logical_and(jnp.logical_not(polar), fits)


def unit_rows():
    return (lax.broadcasted_iota(jnp.int32, (ROWS - HD, 1), 0) == 0).astype(F32)


def plain(acc, qt, keys, values, seen=None):
    s = jnp.dot(keys, qt, preferred_element_type=F32)
    p = jnp.exp2(s).astype(BF16)
    if seen is not None:
        values = jnp.where(seen, values.astype(F32), 0.0).astype(BF16)
    return acc + jnp.dot(values, p, preferred_element_type=F32)


def window_base(j, start):
    return jnp.bitwise_and(j + start + BLOCKS, BLOCKS - 1)


def own_part(qt, base, width, count, k_ref, vt_ref):
    acc = jnp.zeros((ROWS, TOK), F32)
    for at, size in pieces(count * TOK):
        if base is None:
            place, seen = at, None
        else:
            place = pl.multiple_of(base * TOK + at, TOK)
            seen = None
            if at + size > (count - GRAIN + 1) * TOK:
                seen = lax.broadcasted_iota(jnp.int32, (1, size), 1) < width * TOK - at
        acc = plain(acc, qt, k_ref[pl.ds(place, size), :], vt_ref[:, pl.ds(place, size)], seen)
    return acc


def prepare_kernel(scal_ref, recv_ref, k_ref, vt_ref, peak_ref, acc_ref):
    start, width = scal_ref[1], scal_ref[2]
    first, final = scal_ref[0] == 0, scal_ref[0] == scal_ref[4]
    lane = lax.broadcasted_iota(jnp.int32, (1, TOK), 1)
    twice = jnp.logical_or(
        jnp.logical_and(first, lane < EDGE), jnp.logical_and(final, lane >= TOK - EDGE)
    )
    times = jnp.where(twice, 2.0, 1.0).astype(F32)
    ones = (unit_rows() * times).astype(BF16)
    q_most = jnp.zeros((1, TOK), F32)
    k_most = jnp.zeros((1, TOK), F32)
    for j in range(BLOCKS):
        q = recv_ref[j, 0:HD, :].astype(F32)
        k = recv_ref[j, HD : 2 * HD, :]
        kf = k.astype(F32)
        q_most = jnp.maximum(q_most, jnp.sum(q * q, 0, keepdims=True))
        k_most = jnp.maximum(k_most, jnp.sum(kf * kf, 0, keepdims=True))
        v = (recv_ref[j, 2 * HD :, :].astype(F32) * times).astype(BF16)
        kt = k.T
        at = j * TOK
        k_ref[at : at + TOK, :] = kt
        vt_ref[0:HD, at : at + TOK] = v
        vt_ref[HD:, at : at + TOK] = ones
    q_peak = jnp.max(q_most)
    k_peak = jnp.max(k_most)
    peak_ref[0, 0] = q_peak
    peak_ref[0, 1] = k_peak
    safe = q_peak * k_peak < SAFE * SAFE
    polar = jnp.logical_or(first, final)

    @pl.when(jnp.logical_not(jnp.logical_and(safe, polar)))
    def _():
        for at in range(0, OWN, TOK):
            k_ref[OWN + at : OWN + at + TOK, :] = k_ref[at : at + TOK, :]
            vt_ref[:, OWN + at : OWN + at + TOK] = vt_ref[:, at : at + TOK]

    for count, fits in variants(width, polar):

        @pl.when(jnp.logical_and(safe, fits))
        def _(count=count):
            for j in range(PRE):
                base = None if count is None else window_base(j, start)
                qt = recv_ref[j, 0:HD, :]
                acc_ref[j] = own_part(qt, base, width, count or BLOCKS, k_ref, vt_ref)


def prepare(scalars, recv):
    return pl.pallas_call(
        prepare_kernel,
        out_shape=(
            jax.ShapeDtypeStruct((2 * OWN, HD), BF16),
            jax.ShapeDtypeStruct((ROWS, 2 * OWN), BF16),
            jax.ShapeDtypeStruct((1, 2), F32),
            jax.ShapeDtypeStruct((PRE, ROWS, TOK), F32),
        ),
        in_specs=[SMEM, VMEM],
        out_specs=[VMEM, VMEM, SMEM, VMEM],
        compiler_params=pltpu.CompilerParams(vmem_limit_bytes=16 << 20),
        cost_estimate=pl.CostEstimate(flops=10**9, bytes_accessed=6 << 20, transcendentals=0),
        name="prepare",
    )(scalars, recv)


def attend_kernel(scal_ref, peak_ref, recv_ref, k_ref, vt_ref, pre_ref, a_ref, b_ref, out_ref, hk_ref, hvt_ref):
    band, start, width = scal_ref[0], scal_ref[1], scal_ref[2]
    polar = jnp.logical_or(band == 0, band == scal_ref[4])
    k_peak = peak_ref[0, 1]
    for n, ref in enumerate((a_ref, b_ref)):
        rows = slice(n * HALO, (n + 1) * HALO)
        kv = ref[...]
        kf = kv[:, 0:HD].astype(F32)
        k_peak = jnp.maximum(k_peak, jnp.max(jnp.sum(kf * kf, 1, keepdims=True)))
        hk_ref[rows, :] = kv[:, 0:HD]
        hvt_ref[0:HD, rows] = kv.T[HD:]
        hvt_ref[HD:, rows] = jnp.broadcast_to(unit_rows(), (ROWS - HD, HALO)).astype(BF16)
    safe = peak_ref[0, 0] * k_peak < SAFE * SAFE

    def shifted(state, qt, keys, values, seen=None):
        top, acc = state
        s = jnp.dot(keys, qt, preferred_element_type=F32)
        if seen is not None:
            s = jnp.where(seen, s, NEG)
        new = jnp.maximum(top, jnp.max(s, 0, keepdims=True))
        raw = jnp.exp2(s - new)
        if seen is not None:
            raw = jnp.where(seen, raw, 0.0)
        fresh = jnp.dot(values, raw.astype(BF16), preferred_element_type=F32)
        return new, acc * jnp.exp2(top - new) + fresh

    def own(at, size):
        return k_ref[pl.ds(at, size), :], vt_ref[:, pl.ds(at, size)]

    def halo(at, size):
        return hk_ref[pl.ds(at, size), :], hvt_ref[:, pl.ds(at, size)]

    def finish(j, acc):
        out_ref[j] = (acc[0:HD] / acc[HD : HD + 1]).astype(BF16)

    def in_window(edge_key, base):
        block = jnp.bitwise_and(lax.shift_right_logical(edge_key, 5), BLOCKS - 1)
        return jnp.bitwise_and(block - base + BLOCKS, BLOCKS - 1) < width

    def add_halo(j, acc, one_side):
        qt = recv_ref[j, 0:HD, :]
        if one_side:
            acc = plain(acc, qt, *halo(0, HALO))
        else:
            lanes = lax.broadcasted_iota(jnp.int32, (1, 2 * HALO), 1)
            acc = plain(acc, qt, *halo(0, 2 * HALO), in_window(lanes, window_base(j, start)))
        finish(j, acc)

    for one_side, here in ((True, polar), (False, jnp.logical_not(polar))):

        @pl.when(jnp.logical_and(safe, here))
        def _(one_side=one_side):
            for j in range(PRE):
                add_halo(j, pre_ref[j], one_side)

    for count, fits in variants(width, polar):

        @pl.when(jnp.logical_and(safe, fits))
        def _(count=count):
            @pl.loop(PRE, BLOCKS, step=PAIR)
            def _(first):
                for j in (first + n for n in range(PAIR)):
                    base = None if count is None else window_base(j, start)
                    qt = recv_ref[j, 0:HD, :]
                    acc = own_part(qt, base, width, count or BLOCKS, k_ref, vt_ref)
                    add_halo(j, acc, count is None)

    @pl.when(jnp.logical_not(safe))
    def _():
        @pl.loop(0, BLOCKS)
        def _(j):
            qt = recv_ref[j, 0:HD, :]
            base = window_base(j, start)

            def own_step(n, state):
                return shifted(state, qt, *own(pl.multiple_of((base + n) * TOK, TOK), TOK))

            def halo_step(n, state):
                at = pl.multiple_of(n * TOK, TOK)
                row = lax.broadcasted_iota(jnp.int32, (TOK, 1), 0) + at
                return shifted(state, qt, *halo(at, TOK), in_window(row, base))

            state = (jnp.full((1, TOK), NEG, F32), jnp.zeros((ROWS, TOK), F32))
            state = lax.fori_loop(0, width, own_step, state)
            sides = jnp.where(polar, HALO // TOK, 2 * HALO // TOK)
            state = lax.fori_loop(0, sides, halo_step, state)
            finish(j, state[1])


def attend(scalars, peaks, recv, keys, values, pre, side_a, side_b):
    return pl.pallas_call(
        attend_kernel,
        out_shape=jax.ShapeDtypeStruct((BLOCKS, HD, TOK), BF16),
        in_specs=[SMEM, SMEM] + [VMEM] * 6,
        out_specs=VMEM,
        scratch_shapes=[
            pltpu.VMEM((2 * HALO, HD), BF16),
            pltpu.VMEM((ROWS, 2 * HALO), BF16),
        ],
        compiler_params=pltpu.CompilerParams(vmem_limit_bytes=24 << 20),
        cost_estimate=pl.CostEstimate(
            flops=4 * OWN * OWN * HD, bytes_accessed=8 << 20, transcendentals=OWN * OWN
        ),
        name="attend",
    )(scalars, peaks, recv, keys, values, pre, side_a, side_b)


def mix_kernel(att_ref, wo_ref, x_ref, out_ref):
    rows = att_ref[...].T
    width = wo_ref.shape[1]
    cols = width // 2
    for at in range(0, width, cols):
        part = slice(at, at + cols)
        y = jnp.dot(rows, wo_ref[:, part], preferred_element_type=F32)
        y = y + x_ref[:, :, :, part].reshape(y.shape).astype(F32)
        out_ref[:, :, :, part] = y.astype(BF16).reshape(out_ref.shape[:3] + (cols,))


def mix(att, wo, x):
    return pl.pallas_call(
        mix_kernel,
        out_shape=jax.ShapeDtypeStruct(x.shape, BF16),
        in_specs=[VMEM] * 3,
        out_specs=VMEM,
        compiler_params=pltpu.CompilerParams(vmem_limit_bytes=10 << 20),
        name="mix",
    )(att, wo, x)


def swap(value):
    return lax.all_to_all(value, "lon", split_axis=0, concat_axis=0, tiled=True)


def body(tokens, norm_gain, q_weight, k_weight, v_weight, o_weight, band_start, band_width):
    width = tokens.shape[-1]
    n_lat = lax.axis_size("lat")
    band = lax.axis_index("lat")
    scalars = jnp.stack(
        [band, band_start[band], band_width[band], jnp.bitwise_and(band, 1), jnp.int32(n_lat - 1)]
    )
    recv = swap(project(tokens, norm_gain, q_weight, k_weight, v_weight))
    side_a, side_b = edges(scalars, recv)
    pairs_a = [(b, b ^ 1) for b in range(n_lat)]
    pairs_b = [(b, ((b - 1) ^ 1) + 1) for b in range(1, n_lat - 1)]
    side_a = lax.ppermute(side_a, "lat", pairs_a)
    side_b = lax.ppermute(side_b, "lat", pairs_b)
    keys, values, peaks, pre = prepare(scalars, recv)
    att = swap(attend(scalars, peaks, recv, keys, values, pre, side_a, side_b))
    return mix(att.reshape(width, -1), o_weight, tokens)


def solution(mesh):
    placed = (P("lat", "lon", None, None), P(), P(), P(), P(), P(), P(), P())
    return jax.shard_map(
        body, mesh=mesh, in_specs=placed, out_specs=P("lat", "lon", None, None), check_vma=False
    )
```
